256 devices in a mesh: scan: 64 (over x, y_hi, z), tile: 4 (over y_lo, core).
Axes of the slice: x: 4, y: 4 (y_hi: 2, y_lo: 2; y = y_hi * 2 + y_lo), z: 8, core: 2. Of those that a mesh axis runs over, the one named last changes fastest.
Arguments:
- probe_modes: float32 [3072, 256], P(('scan', 'tile')), may hold values from -2.1 to 2.1
- object_tiles: float32 [4, 2, 2, 320, 320], P('tile'), may hold values from -4 to 4
- scan_offsets: int32 [512, 2], P(('scan', 'tile')), may hold values from 0 to 64, as said below
- patch_tiles: int32 [512], P(('scan', 'tile')), may hold values from 0 to 3, as said below
- amplitudes: bfloat16 [512, 256, 256], P(('scan', 'tile')), may hold values from 0.5 to 20
Outputs:
- probe_gradient: float32 [3072, 256], P(('scan', 'tile'))
- object_gradient: float32 [4, 2, 2, 320, 320], P('tile', None, None, 'scan')
The draws below stay inside these ranges and needn't reach their ends.
Inputs may be any that keep to these rules, and one draw needn't show every extreme that they name: `patch_tiles`: each entry names the tile that wholly holds the patch of its position. `scan_offsets`: every patch lies wholly inside its tile.
All inputs are finite; a program needn't handle non-finite values.
Results may differ from the reference program's by a relative error of at most 0.02.
Values sent between devices are 32-bit elements; how exact they have to be, the bound alone decides.
No kernel may reach another device: no remote copies, remote signals or barrier semaphores. Data moves between devices by JAX's collectives and lax.ppermute only.
A program may use at most 128 MiB of HBM per device.

```python
import math
import jax
import jax.numpy as jnp
from jax import lax

PROBE = 256
MODES = 6
SLICES = 2
POS_DEV = 2
TILE_SIDE = 320
TILES = 4
POSITIONS = 512


def heavy_device(key):
    device_total = POSITIONS // POS_DEV
    return jax.random.randint(jax.random.fold_in(key, 7), (), 0, device_total)


def position_device():
    return jnp.arange(POSITIONS, dtype=jnp.int32) // POS_DEV


def draw_patch_tiles(key, part):
    group_width = TILES * POS_DEV
    groups = POSITIONS // group_width
    key_list = jax.random.split(jax.random.fold_in(key, 11), 4)
    favourite = jax.random.randint(key_list[0], (groups, 1), 0, TILES)
    full_group = jax.random.randint(key_list[1], (), 0, groups)
    spread = jax.random.randint(key_list[2], (groups, group_width), 0, TILES)
    coin_flip = jax.random.randint(key_list[3], (groups, group_width), 0, 2)
    chosen = jnp.where(coin_flip == 1, favourite, spread)
    group_index = jnp.arange(groups, dtype=jnp.int32)[:, None]
    chosen = jnp.where(group_index == full_group, favourite, chosen).reshape(POSITIONS)
    heavy = heavy_device(key)
    chosen = jnp.where(position_device() == heavy, heavy % TILES, chosen)
    return chosen.astype(jnp.int32)


def draw_scan_offsets(key, part):
    key_list = jax.random.split(jax.random.fold_in(key, 13), 2)
    offsets = jax.random.randint(key_list[0], (POSITIONS, 2), 0, TILE_SIDE - PROBE + 1)
    heavy = heavy_device(key)
    scan_total = POSITIONS // (POS_DEV * TILES)
    row_count = TILE_SIDE // scan_total
    target = (heavy // TILES + scan_total // 2) % scan_total
    lowest = jnp.maximum(0, (target + 1) * row_count - PROBE)
    highest = jnp.minimum(target * row_count, TILE_SIDE - PROBE)
    planted = jax.random.randint(key_list[1], (POSITIONS,), lowest, highest + 1)
    rows = jnp.where(position_device() == heavy, planted, offsets[:, 0])
    return jnp.stack([rows, offsets[:, 1]], axis=1).astype(jnp.int32)


def draw_amplitudes(key, part):
    key_list = jax.random.split(jax.random.fold_in(key, 17), 2)
    drawn = jax.random.uniform(key_list[0], (POSITIONS, PROBE, PROBE), jnp.float32, 0.5, 2.5)
    strong = jax.random.uniform(key_list[1], (POSITIONS, PROBE, PROBE), jnp.float32, 12.0, 20.0)
    heavy = heavy_device(key)
    chosen = jnp.where((position_device() == heavy)[:, None, None], strong, drawn)
    return chosen.astype(jnp.bfloat16)


def block_scale(own_key, dims, cuts, low, largest):
    loudness = 1.0
    for position, shards_of in cuts:
        draws = jax.random.uniform(jax.random.fold_in(jax.random.fold_in(own_key, 6), position), (shards_of,), jnp.float32, low / len(cuts), largest / len(cuts))
        loudness = loudness * jnp.repeat(jnp.exp(draws), dims[position] // shards_of).reshape((-1,) + (1,) * (len(dims) - 1 - position))
    return loudness


def bell_draw(rng, shape, width, most, shards=(), held_as=jnp.bfloat16):
    entries = width * jax.random.normal(rng, shape, jnp.float32)
    if shards:
        entries = entries * block_scale(rng, shape, shards, -0.22, 0.18)
    return jnp.clip(entries, -most, most).astype(held_as)


def setup_inputs(seed: int = 0) -> dict:
    arg_keys = jax.random.split(jax.random.key(seed), 6)
    probe_modes = bell_draw(arg_keys[0], (2 * MODES * PROBE, PROBE), 0.35, 2.1, ((0, 256),), jnp.float32)
    object_tiles = bell_draw(arg_keys[1], (TILES, SLICES, 2, TILE_SIDE, TILE_SIDE), 0.7, 4.0, ((0, 4),), jnp.float32)
    scan_offsets = draw_scan_offsets(jax.random.fold_in(arg_keys[5], 71), 0)
    patch_tiles = draw_patch_tiles(jax.random.fold_in(arg_keys[5], 71), 0)
    amplitudes = draw_amplitudes(jax.random.fold_in(arg_keys[5], 71), 0)
    return {"probe_modes": probe_modes, "object_tiles": object_tiles, "scan_offsets": scan_offsets, "patch_tiles": patch_tiles, "amplitudes": amplitudes}


def complex_tables(pixels):
    pixel_index = jnp.arange(pixels, dtype=jnp.int32)
    offset = pixel_index[:, None] - pixel_index[None, :]
    chirp_phase = (offset * offset % (2 * pixels)).astype(jnp.float32) * (math.pi / pixels)
    product = (pixel_index[:, None] * pixel_index[None, :] % pixels).astype(jnp.float32) * (2.0 * math.pi / pixels)
    norm_scale = 1.0 / math.sqrt(pixels)
    fresnel = (jnp.stack([jnp.cos(chirp_phase), jnp.sin(chirp_phase)]) * norm_scale).astype(jnp.bfloat16)
    spectral = (jnp.stack([jnp.cos(product), -jnp.sin(product)]) * norm_scale).astype(jnp.bfloat16)
    return (fresnel, spectral)

def multiply_object(exit_wave, object_patch):
    real_part = exit_wave[0] * object_patch[0] - exit_wave[1] * object_patch[1]
    imag_part = exit_wave[0] * object_patch[1] + exit_wave[1] * object_patch[0]
    return jnp.stack([real_part, imag_part])

def left_side(matrix_part, component):
    return jnp.einsum('ij,mjk->mik', matrix_part.astype(jnp.float32), component.astype(jnp.float32), precision=lax.Precision.HIGHEST)

def right_side(component, matrix_part):
    return jnp.einsum('mik,jk->mij', component.astype(jnp.float32), matrix_part.astype(jnp.float32), precision=lax.Precision.HIGHEST)

def left_product(matrix, exit_wave):
    real_part = left_side(matrix[0], exit_wave[0]) - left_side(matrix[1], exit_wave[1])
    imag_part = left_side(matrix[0], exit_wave[1]) + left_side(matrix[1], exit_wave[0])
    return jnp.stack([real_part, imag_part])

def right_product(exit_wave, matrix):
    real_part = right_side(exit_wave[0], matrix[0]) - right_side(exit_wave[1], matrix[1])
    imag_part = right_side(exit_wave[0], matrix[1]) + right_side(exit_wave[1], matrix[0])
    return jnp.stack([real_part, imag_part])

def position_loss(probe_values, patch_values, amplitude, fresnel, spectral):
    exit_wave = probe_values
    layers = patch_values.shape[0]
    for slice_index in range(layers):
        exit_wave = multiply_object(exit_wave, patch_values[slice_index])
        matrix = fresnel if slice_index < layers - 1 else spectral
        rounded = exit_wave.astype(jnp.bfloat16)
        halfway = left_product(matrix, rounded).astype(jnp.bfloat16)
        exit_wave = right_product(halfway, matrix)
    intensity = lax.optimization_barrier(jnp.sum(exit_wave * exit_wave, axis=(0, 1)))
    residue = jnp.sqrt(intensity + 1.0) - amplitude.astype(jnp.float32)
    return jnp.sum(residue * residue)

def reference(probe_modes, object_tiles, scan_offsets, patch_tiles, amplitudes):
    pixels = probe_modes.shape[1]
    layers = object_tiles.shape[1]
    probe_field = probe_modes.astype(jnp.float32).reshape(2, -1, pixels, pixels)
    fresnel, spectral = complex_tables(pixels)

    def one_position(running, inputs):
        probe_total, object_total = running
        offsets, tile_number, amplitude = inputs
        corner = (tile_number.astype(jnp.int32), jnp.int32(0), jnp.int32(0), offsets[0].astype(jnp.int32), offsets[1].astype(jnp.int32))
        extent = (1, layers, 2, pixels, pixels)
        object_patch = lax.dynamic_slice(object_tiles, corner, extent)[0]

        def local_loss(probe_values, patch_values):
            return position_loss(probe_values, patch_values, amplitude, fresnel, spectral)
        misfit, pullback = jax.vjp(local_loss, probe_field, object_patch)
        probe_part, patch_part = pullback(jnp.ones_like(misfit))
        current = lax.dynamic_slice(object_total, corner, extent)
        object_total = lax.dynamic_update_slice(object_total, current + patch_part[None], corner)
        return ((probe_total + probe_part, object_total), None)
    initial = (jnp.zeros_like(probe_field), jnp.zeros(object_tiles.shape, jnp.float32))
    (probe_total, object_total), _ = lax.scan(one_position, initial, (scan_offsets, patch_tiles, amplitudes))
    return (probe_total.reshape(probe_modes.shape), object_total)
```

```python
import functools
import math

import jax
import jax.numpy as jnp
import numpy as np
from jax import lax
from jax.experimental import pallas as pl
from jax.experimental.pallas import tpu as pltpu
from jax.sharding import Mesh
from jax.sharding import PartitionSpec as P

AXES = ("x", "yh", "z", "yl", "c")
ROWS = 128
CUT = 64


def block_matrices(pixels):
    index = np.arange(pixels, dtype=np.int64)
    chirp = ((index[:, None] - index[None, :]) ** 2 % (2 * pixels)) * (math.pi / pixels)
    turn = (index[:, None] * index[None, :] % pixels) * (2.0 * math.pi / pixels)
    scale = 1.0 / math.sqrt(pixels)
    result = []
    for re, im in ((np.cos(chirp), np.sin(chirp)), (np.cos(turn), -np.sin(turn))):
        re, im = (re * scale).astype(jnp.bfloat16), (im * scale).astype(jnp.bfloat16)
        result.append(np.block([[re, im], [-im, re]]))
        result.append(np.block([[re, -im], [im, re]]))
    return np.stack(result)


def dot(a, b):
    return jnp.dot(a, b, preferred_element_type=jnp.float32)


def kernel(
    meta,
    mine,
    other,
    own,
    partner,
    far0,
    far1,
    cross0,
    cross1,
    amplitudes,
    matrices,
    probe_grad,
    canvas,
    probe,
    tiles,
    patch,
    patch_grad,
    wave1,
    wave2,
    tall,
    wide,
    intensity,
    probe_sem,
    tile_sem,
):
    pixels = probe_grad.shape[2] * 2
    half = pixels // 2
    modes = wave1.shape[0]
    positions = tiles.shape[0]
    core = meta[0]
    steps = [slice(i, i + ROWS) for i in range(0, pixels, ROWS)]

    def low(rows):
        return slice(rows.start + pixels, rows.stop + pixels)

    copies = (
        pltpu.make_async_copy(mine, probe.at[core], probe_sem.at[0]),
        pltpu.make_async_copy(other, probe.at[1 - core], probe_sem.at[1]),
    )
    for copy in copies:
        copy.start()
    for n in range(positions):
        kind = meta[1 + 5 * n]
        for source, (first, second) in enumerate(
            ((own.at[0], own.at[1]), (partner.at[0], partner.at[1]), (far0, far1), (cross0, cross1))
        ):

            @pl.when(kind == source)
            def _():
                pltpu.make_async_copy(first, tiles.at[n, 0], tile_sem.at[n, 0]).start()
                pltpu.make_async_copy(second, tiles.at[n, 1], tile_sem.at[n, 1]).start()

    canvas[...] = jnp.zeros_like(canvas)
    for n in range(positions):
        for k in range(2):
            pltpu.make_async_copy(far0, tiles.at[n, k], tile_sem.at[n, k]).wait()
    for copy in copies:
        copy.wait()

    def load_probe(m, part, rows):
        start = pl.multiple_of((part * modes + m) * pixels, pixels) + rows.start
        window = pl.ds(pl.multiple_of(start, ROWS), ROWS)
        return jnp.concatenate([probe[0, window, :], probe[1, window, :]], axis=1)

    def position(n, _):
        base = 1 + 5 * n
        row, down = meta[base + 1], meta[base + 2]
        column, place = meta[base + 3], meta[base + 4]
        up, back = lax.rem(CUT + 8 - down, CUT + 8), lax.rem(384 - column, 384)
        for k in range(2):
            for part in range(2):
                for i in range(0, pixels, CUT):
                    window = pl.ds(pl.multiple_of(row + i, 8), CUT + 8)
                    piece = pltpu.roll(tiles[n, k, part, window, :], up, 0)[:CUT]
                    patch[k, part, i : i + CUT, :] = pltpu.roll(piece, back, 1)[:, :pixels]
        patch_grad[...] = jnp.zeros_like(patch_grad)
        intensity[...] = jnp.zeros_like(intensity)

        def forward(m, _):
            for rows in steps:
                pr, pi = load_probe(m, 0, rows), load_probe(m, 1, rows)
                qr, qi = patch[0, 0, rows, :], patch[0, 1, rows, :]
                tall[rows, :] = (pr * qr - pi * qi).astype(jnp.bfloat16)
                tall[low(rows), :] = (pr * qi + pi * qr).astype(jnp.bfloat16)
            for rows in steps:
                wide[rows, :pixels] = dot(matrices[1, rows, :], tall[...]).astype(jnp.bfloat16)
                wide[rows, pixels:] = dot(matrices[1, low(rows), :], tall[...]).astype(jnp.bfloat16)
            for rows in steps:
                w = dot(wide[rows, :], matrices[0])
                wave1[m, rows, :] = w
                wr, wi = w[:, :pixels], w[:, pixels:]
                qr, qi = patch[1, 0, rows, :], patch[1, 1, rows, :]
                tall[rows, :] = (wr * qr - wi * qi).astype(jnp.bfloat16)
                tall[low(rows), :] = (wr * qi + wi * qr).astype(jnp.bfloat16)
            for rows in steps:
                wide[rows, :pixels] = dot(matrices[3, rows, :], tall[...]).astype(jnp.bfloat16)
                wide[rows, pixels:] = dot(matrices[3, low(rows), :], tall[...]).astype(jnp.bfloat16)
            for rows in steps:
                w = dot(wide[rows, :], matrices[2])
                wave2[m, rows, :] = w
                wr, wi = w[:, :pixels], w[:, pixels:]
                intensity[rows, :] += wr * wr + wi * wi
            return 0

        lax.fori_loop(0, modes, forward, 0)
        for rows in steps:
            measured = amplitudes[n, rows, :].astype(jnp.float32)
            intensity[rows, :] = 2.0 - 2.0 * measured * lax.rsqrt(intensity[rows, :] + 1.0)

        def backward(m, _):
            for rows in steps:
                g = intensity[rows, :]
                w = wave2[m, rows, :]
                d = (w * jnp.concatenate([g, g], axis=1)).astype(jnp.bfloat16)
                d = dot(d, matrices[3]).astype(jnp.bfloat16)
                tall[rows, :] = d[:, :pixels]
                tall[low(rows), :] = d[:, pixels:]
            for rows in steps:
                dr = dot(matrices[2, rows, :], tall[...])
                di = dot(matrices[2, low(rows), :], tall[...])
                dr = dr.astype(jnp.bfloat16).astype(jnp.float32)
                di = di.astype(jnp.bfloat16).astype(jnp.float32)
                wr, wi = wave1[m, rows, :pixels], wave1[m, rows, pixels:]
                patch_grad[1, 0, rows, :] += dr * wr + di * wi
                patch_grad[1, 1, rows, :] += di * wr - dr * wi
                qr, qi = patch[1, 0, rows, :], patch[1, 1, rows, :]
                wide[rows, :pixels] = (dr * qr + di * qi).astype(jnp.bfloat16)
                wide[rows, pixels:] = (di * qr - dr * qi).astype(jnp.bfloat16)
            for rows in steps:
                d = dot(wide[rows, :], matrices[1]).astype(jnp.bfloat16)
                tall[rows, :] = d[:, :pixels]
                tall[low(rows), :] = d[:, pixels:]
            for rows in steps:
                dr = dot(matrices[0, rows, :], tall[...])
                di = dot(matrices[0, low(rows), :], tall[...])
                dr = dr.astype(jnp.bfloat16).astype(jnp.float32)
                di = di.astype(jnp.bfloat16).astype(jnp.float32)
                pr, pi = load_probe(m, 0, rows), load_probe(m, 1, rows)
                patch_grad[0, 0, rows, :] += dr * pr + di * pi
                patch_grad[0, 1, rows, :] += di * pr - dr * pi
                qr, qi = patch[0, 0, rows, :], patch[0, 1, rows, :]
                for part, value in enumerate((dr * qr + di * qi, di * qr - dr * qi)):
                    start = pl.multiple_of((part * modes + m) * pixels, pixels) + rows.start
                    window = pl.ds(pl.multiple_of(start, ROWS), ROWS)
                    for side in range(2):
                        piece = value[:, side * half : (side + 1) * half]

                        @pl.when(n == 0)
                        def _():
                            probe_grad[side, window, :] = piece

                        @pl.when(n > 0)
                        def _():
                            probe_grad[side, window, :] += piece
            return 0

        lax.fori_loop(0, modes, backward, 0)
        for k in range(2):
            for part in range(2):
                lane = (k * 2 + part) * 320 - part * 64
                for i in range(0, pixels, CUT):
                    piece = patch_grad[k, part, i : i + CUT, :]
                    piece = jnp.pad(piece, ((0, 8), (0, 128)))
                    piece = pltpu.roll(pltpu.roll(piece, column + part * 64, 1), down, 0)
                    window = pl.ds(pl.multiple_of(row + i, 8), CUT + 8)
                    canvas[place, window, lane : lane + 384] += piece
        return 0

    lax.fori_loop(0, positions, position, 0)


def device_gradients(meta, mine, other, tile_parts, amplitudes):
    pixels = 2 * mine.shape[1]
    modes = mine.shape[0] // (2 * pixels)
    positions = amplitudes.shape[0]
    whole = pl.BlockSpec(memory_space=pltpu.VMEM)
    there = pl.BlockSpec(memory_space=pl.ANY)
    scratch = [
        pltpu.VMEM((2, mine.shape[0], half_of(pixels)), jnp.float32),
        pltpu.VMEM((positions, 2, 2, 320, 384), jnp.float32),
        pltpu.VMEM((2, 2, pixels, pixels), jnp.float32),
        pltpu.VMEM((2, 2, pixels, pixels), jnp.float32),
        pltpu.VMEM((modes, pixels, 2 * pixels), jnp.float32),
        pltpu.VMEM((modes, pixels, 2 * pixels), jnp.float32),
        pltpu.VMEM((2 * pixels, pixels), jnp.bfloat16),
        pltpu.VMEM((pixels, 2 * pixels), jnp.bfloat16),
        pltpu.VMEM((pixels, pixels), jnp.float32),
        pltpu.SemaphoreType.DMA((2,)),
        pltpu.SemaphoreType.DMA((positions, 2)),
    ]
    flops = positions * modes * 8 * 4 * 2 * pixels**3
    return pl.pallas_call(
        kernel,
        out_shape=(
            jax.ShapeDtypeStruct((2, mine.shape[0], half_of(pixels)), jnp.float32),
            jax.ShapeDtypeStruct((4, 320, 1280), jnp.float32),
        ),
        in_specs=[pl.BlockSpec(memory_space=pltpu.SMEM)] + [there] * 8 + [whole] * 2,
        out_specs=(whole, whole),
        scratch_shapes=scratch,
        cost_estimate=pl.CostEstimate(flops=flops, bytes_accessed=20_000_000, transcendentals=0),
        compiler_params=pltpu.CompilerParams(vmem_limit_bytes=56 * 1024 * 1024),
        name="gradients",
    )(meta, mine, other, *tile_parts, amplitudes, jnp.asarray(block_matrices(pixels)))


def half_of(pixels):
    return pixels // 2


def exchange(value, axes):
    return lax.all_to_all(value, axes, split_axis=0, concat_axis=0, tiled=True)


def spread(value, axes, count):
    return exchange(jnp.broadcast_to(value[None], (count,) + value.shape), axes)


def reduce_over(value, axes):
    return jnp.sum(exchange(value, axes), axis=0)


def shift(value, axes, count, by):
    return lax.ppermute(value, axes, [(i, (i + by) % count) for i in range(count)])


def body(probe_modes, object_tiles, scan_offsets, patch_tiles, amplitudes):
    core, low_y = lax.axis_index("c"), lax.axis_index("yl")
    pixels = probe_modes.shape[1]
    own_rows = probe_modes.shape[0]
    half = pixels // 2

    padded = jnp.pad(object_tiles[0], ((0, 0), (0, 0), (0, 0), (0, 64)))
    far0 = shift(padded[0], ("yh", "yl"), 4, 1)
    far1 = shift(padded[1], ("yh", "yl"), 4, 3)
    partner = shift(padded, "c", 2, 1)

    columns = jnp.stack([probe_modes[:, :half], probe_modes[:, half:]])
    pair = exchange(columns, "c").reshape(2 * own_rows, half)
    block = spread(pair, ("z", "yl"), 16).reshape(32 * own_rows, half)
    mine = spread(block, ("x", "yh"), 8).reshape(256 * own_rows, half)
    other = shift(mine, "c", 2, 1)
    cross0 = shift(far0, "c", 2, 1)
    cross1 = shift(far1, "c", 2, 1)

    tile_y, tile_core = patch_tiles // 2, patch_tiles % 2
    kind = (tile_y ^ low_y) * 2 + (tile_core ^ core)
    aligned = jnp.minimum(scan_offsets[:, 0] // 8 * 8, 56)
    down = scan_offsets[:, 0] - aligned
    entries = jnp.stack([kind, aligned, down, scan_offsets[:, 1], tile_core * 2 + tile_y], axis=1)
    meta = jnp.concatenate([core.reshape(1), entries.reshape(-1)]).astype(jnp.int32)

    probe_part, canvas = device_gradients(
        meta, mine, other, (padded, partner, far0, far1, cross0, cross1), amplitudes
    )

    canvas = reduce_over(canvas.reshape(2, 640, 1280), "c")
    canvas = reduce_over(canvas.reshape(16, 40, 1280), ("yl", "x", "yh"))
    canvas = reduce_over(canvas.reshape(8, 5, 1280), "z")
    object_gradient = canvas.reshape(5, 2, 2, 320).transpose(1, 2, 0, 3)[None]

    probe_part = reduce_over(probe_part, "c")
    probe_part = reduce_over(probe_part.reshape(8, 32 * own_rows, half), ("x", "yh"))
    probe_part = reduce_over(probe_part.reshape(16, 2 * own_rows, half), ("z", "yl"))
    columns = exchange(probe_part.reshape(2, own_rows, half), "c")
    probe_gradient = jnp.concatenate([columns[0], columns[1]], axis=1)
    return (probe_gradient, object_gradient)


def solution(mesh):
    fine = Mesh(mesh.devices.reshape(4, 2, 8, 2, 2), AXES)
    scan, tile = AXES[:3], AXES[3:]
    placed = (
        P(AXES, None),
        P(tile, None, None, None, None),
        P(AXES, None),
        P(AXES),
        P(AXES, None, None),
    )
    return jax.shard_map(
        body,
        mesh=fine,
        in_specs=placed,
        out_specs=(P(AXES, None), P(tile, None, None, scan, None)),
        check_vma=False,
    )
```

```python
import math

import jax
import jax.numpy as jnp
import numpy as np
from jax import lax
from jax.experimental import pallas as pl
from jax.experimental.pallas import tpu as pltpu
from jax.sharding import Mesh
from jax.sharding import PartitionSpec as P

AXES = ("x", "yh", "z", "yl", "c")
ROWS = 128
CUT = 64


def block_matrices(pixels):
    index = np.arange(pixels, dtype=np.int64)
    chirp = ((index[:, None] - index[None, :]) ** 2 % (2 * pixels)) * (math.pi / pixels)
    turn = (index[:, None] * index[None, :] % pixels) * (2.0 * math.pi / pixels)
    scale = 1.0 / math.sqrt(pixels)
    result = []
    for re, im in ((np.cos(chirp), np.sin(chirp)), (np.cos(turn), -np.sin(turn))):
        re, im = (re * scale).astype(jnp.bfloat16), (im * scale).astype(jnp.bfloat16)
        result.append(np.block([[re, im], [-im, re]]))
        result.append(np.block([[re, -im], [im, re]]))
    return np.stack(result)


def dot(a, b):
    return jnp.dot(a, b, preferred_element_type=jnp.float32)


def kernel(
    meta,
    mine,
    other,
    own,
    partner,
    far0,
    far1,
    cross0,
    cross1,
    amplitudes,
    matrices,
    keep,
    send,
    probe_grad,
    canvas,
    probe,
    tiles,
    patch,
    patch_grad,
    wave1,
    wave2,
    tall,
    wide,
    intensity,
    probe_sem,
    tile_sem,
    out_sem,
):
    pixels = probe_grad.shape[2] * 2
    half = pixels // 2
    modes = wave1.shape[0]
    positions = tiles.shape[0]
    core = meta[0]
    steps = [slice(i, i + ROWS) for i in range(0, pixels, ROWS)]

    def low(rows):
        return slice(rows.start + pixels, rows.stop + pixels)

    blocks = probe.reshape(2, 8, 8, 2, 24, half)
    copies = [
        pltpu.make_async_copy(source.at[:, y], blocks.at[side, :, :, y], probe_sem.at[i, y])
        for i, (source, side) in enumerate(((mine, core), (other, 1 - core)))
        for y in range(2)
    ]
    for copy in copies:
        copy.start()
    grad_blocks = probe_grad.reshape(2, 8, 8, 2, 24, half)
    probe_out = [
        pltpu.make_async_copy(
            grad_blocks.at[side, :, z, y],
            target.at[8 * y : 8 * y + 8, 400 + 24 * z : 424 + 24 * z, :],
            out_sem.at[i, y, z],
        )
        for i, (target, side) in enumerate(((keep, core), (send, 1 - core)))
        for y in range(2)
        for z in range(8)
    ]
    canvas_blocks = canvas.reshape(4, 8, 40, 1280)
    canvas_out = [
        pltpu.make_async_copy(
            canvas_blocks.at[2 * i + y, :, :, 128 * j : 128 * j + 128],
            target.at[8 * y : 8 * y + 8, 40 * j : 40 * j + 40, :],
            out_sem.at[i, y, 8 + j],
        )
        for i, target in enumerate((keep, send))
        for y in range(2)
        for j in range(10)
    ]
    for n in range(positions):
        kind = meta[1 + 5 * n]
        for source, (first, second) in enumerate(
            ((own.at[0], own.at[1]), (partner.at[0], partner.at[1]), (far0, far1), (cross0, cross1))
        ):

            @pl.when(kind == source)
            def _():
                pltpu.make_async_copy(first, tiles.at[n, 0], tile_sem.at[n, 0]).start()
                pltpu.make_async_copy(second, tiles.at[n, 1], tile_sem.at[n, 1]).start()

    canvas[...] = jnp.zeros_like(canvas)
    for n in range(positions):
        for k in range(2):
            pltpu.make_async_copy(far0, tiles.at[n, k], tile_sem.at[n, k]).wait()
    for copy in copies:
        copy.wait()

    def load_probe(m, part, rows):
        start = pl.multiple_of((part * modes + m) * pixels, pixels) + rows.start
        window = pl.ds(pl.multiple_of(start, ROWS), ROWS)
        return jnp.concatenate([probe[0, window, :], probe[1, window, :]], axis=1)

    def position(n, _):
        base = 1 + 5 * n
        row, down = meta[base + 1], meta[base + 2]
        column, place = meta[base + 3], meta[base + 4]
        up, back = lax.rem(CUT + 8 - down, CUT + 8), lax.rem(384 - column, 384)
        for k in range(2):
            for part in range(2):
                for i in range(0, pixels, CUT):
                    window = pl.ds(pl.multiple_of(row + i, 8), CUT + 8)
                    piece = pltpu.roll(tiles[n, k, part, window, :], up, 0)[:CUT]
                    patch[k, part, i : i + CUT, :] = pltpu.roll(piece, back, 1)[:, :pixels]
        patch_grad[...] = jnp.zeros_like(patch_grad)
        intensity[...] = jnp.zeros_like(intensity)

        def forward(m, _):
            for rows in steps:
                pr, pi = load_probe(m, 0, rows), load_probe(m, 1, rows)
                qr, qi = patch[0, 0, rows, :], patch[0, 1, rows, :]
                tall[rows, :] = (pr * qr - pi * qi).astype(jnp.bfloat16)
                tall[low(rows), :] = (pr * qi + pi * qr).astype(jnp.bfloat16)
            for rows in steps:
                wide[rows, :pixels] = dot(matrices[1, rows, :], tall[...]).astype(jnp.bfloat16)
                wide[rows, pixels:] = dot(matrices[1, low(rows), :], tall[...]).astype(jnp.bfloat16)
            for rows in steps:
                w = dot(wide[rows, :], matrices[0])
                wave1[m, rows, :] = w
                wr, wi = w[:, :pixels], w[:, pixels:]
                qr, qi = patch[1, 0, rows, :], patch[1, 1, rows, :]
                tall[rows, :] = (wr * qr - wi * qi).astype(jnp.bfloat16)
                tall[low(rows), :] = (wr * qi + wi * qr).astype(jnp.bfloat16)
            for rows in steps:
                wide[rows, :pixels] = dot(matrices[3, rows, :], tall[...]).astype(jnp.bfloat16)
                wide[rows, pixels:] = dot(matrices[3, low(rows), :], tall[...]).astype(jnp.bfloat16)
            for rows in steps:
                w = dot(wide[rows, :], matrices[2])
                wave2[m, rows, :] = w
                wr, wi = w[:, :pixels], w[:, pixels:]
                intensity[rows, :] += wr * wr + wi * wi
            return 0

        lax.fori_loop(0, modes, forward, 0)
        for rows in steps:
            measured = amplitudes[n, rows, :].astype(jnp.float32)
            intensity[rows, :] = 2.0 - 2.0 * measured * lax.rsqrt(intensity[rows, :] + 1.0)

        def backward(m, _):
            for rows in steps:
                g = intensity[rows, :]
                w = wave2[m, rows, :]
                d = (w * jnp.concatenate([g, g], axis=1)).astype(jnp.bfloat16)
                d = dot(d, matrices[3]).astype(jnp.bfloat16)
                tall[rows, :] = d[:, :pixels]
                tall[low(rows), :] = d[:, pixels:]
            for rows in steps:
                dr = dot(matrices[2, rows, :], tall[...])
                di = dot(matrices[2, low(rows), :], tall[...])
                dr = dr.astype(jnp.bfloat16).astype(jnp.float32)
                di = di.astype(jnp.bfloat16).astype(jnp.float32)
                wr, wi = wave1[m, rows, :pixels], wave1[m, rows, pixels:]
                patch_grad[1, 0, rows, :] += dr * wr + di * wi
                patch_grad[1, 1, rows, :] += di * wr - dr * wi
                qr, qi = patch[1, 0, rows, :], patch[1, 1, rows, :]
                wide[rows, :pixels] = (dr * qr + di * qi).astype(jnp.bfloat16)
                wide[rows, pixels:] = (di * qr - dr * qi).astype(jnp.bfloat16)
            for rows in steps:
                d = dot(wide[rows, :], matrices[1]).astype(jnp.bfloat16)
                tall[rows, :] = d[:, :pixels]
                tall[low(rows), :] = d[:, pixels:]
            for rows in steps:
                dr = dot(matrices[0, rows, :], tall[...])
                di = dot(matrices[0, low(rows), :], tall[...])
                dr = dr.astype(jnp.bfloat16).astype(jnp.float32)
                di = di.astype(jnp.bfloat16).astype(jnp.float32)
                pr, pi = load_probe(m, 0, rows), load_probe(m, 1, rows)
                patch_grad[0, 0, rows, :] += dr * pr + di * pi
                patch_grad[0, 1, rows, :] += di * pr - dr * pi
                qr, qi = patch[0, 0, rows, :], patch[0, 1, rows, :]
                for part, value in enumerate((dr * qr + di * qi, di * qr - dr * qi)):
                    start = pl.multiple_of((part * modes + m) * pixels, pixels) + rows.start
                    window = pl.ds(pl.multiple_of(start, ROWS), ROWS)
                    for side in range(2):
                        piece = value[:, side * half : (side + 1) * half]

                        @pl.when(n == 0)
                        def _():
                            probe_grad[side, window, :] = piece

                        @pl.when(n > 0)
                        def _():
                            probe_grad[side, window, :] += piece
            return 0

        lax.fori_loop(0, modes, backward, 0)

        @pl.when(n == positions - 1)
        def _():
            for copy in probe_out:
                copy.start()

        for k in range(2):
            for part in range(2):
                lane = (k * 2 + part) * 320 - part * 64
                for i in range(0, pixels, CUT):
                    piece = patch_grad[k, part, i : i + CUT, :]
                    piece = jnp.pad(piece, ((0, 8), (0, 128)))
                    piece = pltpu.roll(pltpu.roll(piece, column + part * 64, 1), down, 0)
                    window = pl.ds(pl.multiple_of(row + i, 8), CUT + 8)
                    canvas[place, window, lane : lane + 384] += piece
        return 0

    lax.fori_loop(0, positions, position, 0)
    for copy in canvas_out:
        copy.start()
    for copy in probe_out + canvas_out:
        copy.wait()


def device_gradients(meta, mine, other, tile_parts, amplitudes):
    pixels = 2 * mine.shape[-1]
    rows = math.prod(mine.shape[:-1])
    modes = rows // (2 * pixels)
    positions = amplitudes.shape[0]
    whole = pl.BlockSpec(memory_space=pltpu.VMEM)
    there = pl.BlockSpec(memory_space=pl.ANY)
    scratch = [
        pltpu.VMEM((2, rows, pixels // 2), jnp.float32),
        pltpu.VMEM((4, 320, 1280), jnp.float32),
        pltpu.VMEM((2, rows, pixels // 2), jnp.float32),
        pltpu.VMEM((positions, 2, 2, 320, 384), jnp.float32),
        pltpu.VMEM((2, 2, pixels, pixels), jnp.float32),
        pltpu.VMEM((2, 2, pixels, pixels), jnp.float32),
        pltpu.VMEM((modes, pixels, 2 * pixels), jnp.float32),
        pltpu.VMEM((modes, pixels, 2 * pixels), jnp.float32),
        pltpu.VMEM((2 * pixels, pixels), jnp.bfloat16),
        pltpu.VMEM((pixels, 2 * pixels), jnp.bfloat16),
        pltpu.VMEM((pixels, pixels), jnp.float32),
        pltpu.SemaphoreType.DMA((2, 2)),
        pltpu.SemaphoreType.DMA((positions, 2)),
        pltpu.SemaphoreType.DMA((2, 2, 18)),
    ]
    flops = positions * modes * 8 * 4 * 2 * pixels**3
    return pl.pallas_call(
        kernel,
        out_shape=(jax.ShapeDtypeStruct((16, 592, 128), jnp.float32),) * 2,
        in_specs=[pl.BlockSpec(memory_space=pltpu.SMEM)] + [there] * 8 + [whole] * 2,
        out_specs=(there, there),
        scratch_shapes=scratch,
        cost_estimate=pl.CostEstimate(flops=flops, bytes_accessed=20_000_000, transcendentals=0),
        compiler_params=pltpu.CompilerParams(vmem_limit_bytes=56 * 1024 * 1024),
        name="gradients",
    )(meta, mine, other, *tile_parts, amplitudes, jnp.asarray(block_matrices(pixels)))


def exchange(value, axes):
    return lax.all_to_all(value, axes, split_axis=0, concat_axis=0, tiled=True)


def spread(value, axes, count):
    return exchange(jnp.broadcast_to(value[None], (count,) + value.shape), axes)


def reduce_over(value, axes):
    return jnp.sum(exchange(value, axes), axis=0)


def shift(value, axes, count, by):
    return lax.ppermute(value, axes, [(i, (i + by) % count) for i in range(count)])


def device_body(probe_modes, object_tiles, scan_offsets, patch_tiles, amplitudes):
    core, low_y = lax.axis_index("c"), lax.axis_index("yl")
    own_rows, pixels = probe_modes.shape
    half = pixels // 2

    padded = jnp.pad(object_tiles[0], ((0, 0), (0, 0), (0, 0), (0, 64)))
    far0 = shift(padded[0], ("yh", "yl"), 4, 1)
    far1 = shift(padded[1], ("yh", "yl"), 4, 3)
    partner = shift(padded, "c", 2, 1)
    cross0 = shift(far0, "c", 2, 1)
    cross1 = shift(far1, "c", 2, 1)

    columns = jnp.stack([probe_modes[:, :half], probe_modes[:, half:]])
    pair = exchange(columns, "c").reshape(2 * own_rows, half)
    block = spread(pair, "z", 8)
    mine = spread(block, ("x", "yh", "yl"), 16).reshape(8, 2, 8, 2 * own_rows, half)
    other = shift(mine, "c", 2, 1)

    tile_y, tile_core = patch_tiles // 2, patch_tiles % 2
    kind = (tile_core ^ core) + 2 * (tile_y ^ low_y)
    aligned = jnp.minimum(scan_offsets[:, 0] // 8 * 8, 56)
    down = scan_offsets[:, 0] - aligned
    place = 2 * (tile_core ^ core) + tile_y
    entries = jnp.stack([kind, aligned, down, scan_offsets[:, 1], place], axis=1)
    meta = jnp.concatenate([core.reshape(1), entries.reshape(-1)]).astype(jnp.int32)

    keep, send = device_gradients(
        meta, mine, other, (padded, partner, far0, far1, cross0, cross1), amplitudes
    )

    total = keep + shift(send, "c", 2, 1)
    total = reduce_over(total, ("yl", "x", "yh"))
    objects = total[:400].reshape(10, 8, 5, 128).transpose(1, 0, 2, 3).reshape(8, 50, 128)
    total = reduce_over(jnp.concatenate([objects, total[400:].reshape(8, 24, 128)], axis=1), "z")
    object_gradient = total[:50].reshape(10, 5, 128).transpose(1, 0, 2).reshape(5, 2, 2, 320)
    object_gradient = object_gradient.transpose(1, 2, 0, 3)[None]
    columns = exchange(total[50:].reshape(2, own_rows, half), "c")
    probe_gradient = jnp.concatenate([columns[0], columns[1]], axis=1)
    return (probe_gradient, object_gradient)


def solution(mesh):
    fine = Mesh(mesh.devices.reshape(4, 2, 8, 2, 2), AXES)
    scan, tile = AXES[:3], AXES[3:]
    placed = (
        P(AXES, None),
        P(tile, None, None, None, None),
        P(AXES, None),
        P(AXES),
        P(AXES, None, None),
    )
    return jax.shard_map(
        device_body,
        mesh=fine,
        in_specs=placed,
        out_specs=(P(AXES, None), P(tile, None, None, scan, None)),
        check_vma=False,
    )
```

```python
import math

import jax
import jax.numpy as jnp
import numpy as np
from jax import lax
from jax.experimental import pallas as pl
from jax.experimental.pallas import tpu as pltpu
from jax.sharding import Mesh
from jax.sharding import PartitionSpec as P

AXES = ("x", "yh", "z", "yl", "c")
ROWS = 256
CUT = 64
GROUP = 2


def block_matrices(pixels):
    index = np.arange(pixels, dtype=np.int64)
    chirp = ((index[:, None] - index[None, :]) ** 2 % (2 * pixels)) * (math.pi / pixels)
    turn = (index[:, None] * index[None, :] % pixels) * (2.0 * math.pi / pixels)
    scale = 1.0 / math.sqrt(pixels)
    result = []
    for re, im in ((np.cos(chirp), np.sin(chirp)), (np.cos(turn), -np.sin(turn))):
        re, im = (re * scale).astype(jnp.bfloat16), (im * scale).astype(jnp.bfloat16)
        result.append(np.block([[re, im], [-im, re]]))
        result.append(np.block([[re, -im], [im, re]]))
    return np.stack(result)


def dot(a, b):
    return jnp.dot(a, b, preferred_element_type=jnp.float32)


def shift_left(value, lanes, sublanes):
    groups = value.shape[0] // 8
    value = pltpu.roll(value.reshape(groups, 8, 384), lax.rem(8 - sublanes, 8), 1)
    index = lax.broadcasted_iota(jnp.int32, (groups - 1, 8, 384), 1)
    value = jnp.where(index < 8 - sublanes, value[:-1], value[1:]).reshape(8 * groups - 8, 384)
    turn = lax.rem(128 - lanes, 128)
    parts = [pltpu.roll(value[:, a : a + 128], turn, 1) for a in (0, 128, 256)]
    index = lax.broadcasted_iota(jnp.int32, parts[0].shape, 1)
    keep = index < 128 - lanes
    return jnp.concatenate([jnp.where(keep, a, b) for a, b in zip(parts, parts[1:])], axis=1)


def shift_right(value, lanes, sublanes):
    groups = value.shape[0] // 8
    turn = lax.rem(lanes, 128)
    zero = jnp.zeros((value.shape[0], 128), jnp.float32)
    parts = [zero] + [pltpu.roll(value[:, a : a + 128], turn, 1) for a in (0, 128)] + [zero]
    index = lax.broadcasted_iota(jnp.int32, zero.shape, 1)
    moved = index < lanes
    value = jnp.concatenate([jnp.where(moved, a, b) for a, b in zip(parts, parts[1:])], axis=1)
    value = pltpu.roll(value.reshape(groups, 8, 384), lax.rem(sublanes, 8), 1)
    zero = jnp.zeros((1, 8, 384), jnp.float32)
    above, below = jnp.concatenate([zero, value]), jnp.concatenate([value, zero])
    index = lax.broadcasted_iota(jnp.int32, above.shape, 1)
    return jnp.where(index < sublanes, above, below).reshape(8 * groups + 8, 384)


def kernel(
    offsets,
    chosen,
    mine,
    other,
    own,
    partner,
    far0,
    far1,
    cross0,
    cross1,
    amplitudes,
    matrices,
    keep,
    send,
    probe_grad,
    canvas,
    probe,
    tiles,
    packed,
    patch,
    patch_grad,
    wave1,
    wave2,
    tall,
    wide,
    intensity,
    probe_sem,
    tile_sem,
    out_sem,
):
    half = probe_grad.shape[2]
    pixels = 2 * half
    modes = wave1.shape[0]
    positions = tiles.shape[0]
    core, low_y = lax.axis_index("c"), lax.axis_index("yl")
    steps = [slice(i, i + ROWS) for i in range(0, pixels, ROWS)]
    lanes_of = range(GROUP)

    def low(rows):
        return slice(rows.start + pixels, rows.stop + pixels)

    copies = [
        pltpu.make_async_copy(source, packed.at[side], probe_sem.at[i])
        for i, (source, side) in enumerate(((mine, core), (other, 1 - core)))
    ]
    for copy in copies:
        copy.start()
    grad_blocks = packed.reshape(2, 8, 8, 2, 24, half)
    probe_out = [
        pltpu.make_async_copy(
            grad_blocks.at[side, :, z, y],
            target.at[8 * y : 8 * y + 8, 400 + 24 * z : 424 + 24 * z, :],
            out_sem.at[i, y, z],
        )
        for i, (target, side) in enumerate(((keep, core), (send, 1 - core)))
        for y in range(2)
        for z in range(8)
    ]
    canvas_blocks = canvas.reshape(4, 8, 40, 1280)
    canvas_out = [
        pltpu.make_async_copy(
            canvas_blocks.at[2 * i + y, :, :, 128 * j : 128 * j + 128],
            target.at[8 * y : 8 * y + 8, 40 * j : 40 * j + 40, :],
            out_sem.at[i, y, 8 + j],
        )
        for i, target in enumerate((keep, send))
        for y in range(2)
        for j in range(10)
    ]
    for n in range(positions):
        tile = chosen[n]
        kind = 2 * (lax.div(tile, 2) ^ low_y) + (lax.rem(tile, 2) ^ core)
        for source, (first, second) in enumerate(
            ((own.at[0], own.at[1]), (partner.at[0], partner.at[1]), (far0, far1), (cross0, cross1))
        ):

            @pl.when(kind == source)
            def _():
                pltpu.make_async_copy(first, tiles.at[n, 0], tile_sem.at[n, 0]).start()
                pltpu.make_async_copy(second, tiles.at[n, 1], tile_sem.at[n, 1]).start()

    canvas[...] = jnp.zeros_like(canvas)
    probe_grad[...] = jnp.zeros_like(probe_grad)
    for n in range(positions):
        for k in range(2):
            pltpu.make_async_copy(far0, tiles.at[n, k], tile_sem.at[n, k]).wait()
    for copy in copies:
        copy.wait()
    upper = lax.broadcasted_iota(jnp.int32, (8, half), 0) < 4

    def unpack(block, _):
        start = pl.multiple_of(24 * block, 8)
        for side in range(2):
            probe[side, pl.ds(start, 8), :] = packed[0, block, 8 * side : 8 * side + 8, :]
            probe[side, pl.ds(start + 16, 8), :] = packed[1, block, 8 * side : 8 * side + 8, :]
        a, b = packed[0, block, 16:24, :], packed[1, block, 16:24, :]
        probe[0, pl.ds(start + 8, 8), :] = jnp.where(upper, a, b)
        probe[1, pl.ds(start + 8, 8), :] = pltpu.roll(jnp.where(upper, b, a), 4, 0)
        return 0

    def pack(block, _):
        start = pl.multiple_of(24 * block, 8)
        for side in range(2):
            packed[0, block, 8 * side : 8 * side + 8, :] = probe_grad[side, pl.ds(start, 8), :]
            packed[1, block, 8 * side : 8 * side + 8, :] = probe_grad[side, pl.ds(start + 16, 8), :]
        a = probe_grad[0, pl.ds(start + 8, 8), :]
        b = pltpu.roll(probe_grad[1, pl.ds(start + 8, 8), :], 4, 0)
        packed[0, block, 16:24, :] = jnp.where(upper, a, b)
        packed[1, block, 16:24, :] = jnp.where(upper, b, a)
        return 0

    lax.fori_loop(0, packed.shape[1], unpack, 0, unroll=8)

    def window_of(m, part, rows):
        start = pl.multiple_of((part * modes + m) * pixels, pixels) + rows.start
        return pl.ds(pl.multiple_of(start, ROWS), ROWS)

    def load_probe(m, part, rows):
        window = window_of(m, part, rows)
        return jnp.concatenate([probe[0, window, :], probe[1, window, :]], axis=1)

    def position(n, _):
        row, column, tile = offsets[n, 0], offsets[n, 1], chosen[n]
        base = jnp.minimum(lax.div(row, 8) * 8, 56)
        down = row - base
        place = 2 * (lax.rem(tile, 2) ^ core) + lax.div(tile, 2)
        for k in range(2):
            for part in range(2):
                for i in range(0, pixels, CUT):
                    window = pl.ds(pl.multiple_of(base + i, 8), CUT + 8)
                    patch[k, part, i : i + CUT, :] = shift_left(tiles[n, k, part, window, :], column, down)
        patch_grad[...] = jnp.zeros_like(patch_grad)
        intensity[...] = jnp.zeros_like(intensity)

        def forward(group, _):
            first = group * GROUP
            for j in lanes_of:
                for rows in steps:
                    pr, pi = load_probe(first + j, 0, rows), load_probe(first + j, 1, rows)
                    qr, qi = patch[0, 0, rows, :], patch[0, 1, rows, :]
                    tall[j, 0, rows, :] = (pr * qr - pi * qi).astype(jnp.bfloat16)
                    tall[j, 0, low(rows), :] = (pr * qi + pi * qr).astype(jnp.bfloat16)
            for j in lanes_of:
                for rows in steps:
                    a = dot(matrices[1, rows, :], tall[j, 0])
                    wide[j, 0, rows, :pixels] = a.astype(jnp.bfloat16)
                    a = dot(matrices[1, low(rows), :], tall[j, 0])
                    wide[j, 0, rows, pixels:] = a.astype(jnp.bfloat16)
            for j in lanes_of:
                for rows in steps:
                    w = dot(wide[j, 0, rows, :], matrices[0])
                    wave1[first + j, rows, :] = w
                    wr, wi = w[:, :pixels], w[:, pixels:]
                    qr, qi = patch[1, 0, rows, :], patch[1, 1, rows, :]
                    tall[j, 1, rows, :] = (wr * qr - wi * qi).astype(jnp.bfloat16)
                    tall[j, 1, low(rows), :] = (wr * qi + wi * qr).astype(jnp.bfloat16)
            for j in lanes_of:
                for rows in steps:
                    a = dot(matrices[3, rows, :], tall[j, 1])
                    wide[j, 1, rows, :pixels] = a.astype(jnp.bfloat16)
                    a = dot(matrices[3, low(rows), :], tall[j, 1])
                    wide[j, 1, rows, pixels:] = a.astype(jnp.bfloat16)
            for j in lanes_of:
                for rows in steps:
                    w = dot(wide[j, 1, rows, :], matrices[2])
                    wave2[first + j, rows, :] = w
                    wr, wi = w[:, :pixels], w[:, pixels:]
                    intensity[rows, :] += wr * wr + wi * wi
            return 0

        lax.fori_loop(0, modes // GROUP, forward, 0)
        for rows in steps:
            measured = amplitudes[n, rows, :].astype(jnp.float32)
            intensity[rows, :] = 2.0 - 2.0 * measured * lax.rsqrt(intensity[rows, :] + 1.0)

        def backward(group, _):
            first = group * GROUP
            for j in lanes_of:
                for rows in steps:
                    g = intensity[rows, :]
                    w = wave2[first + j, rows, :]
                    d = (w * jnp.concatenate([g, g], axis=1)).astype(jnp.bfloat16)
                    d = dot(d, matrices[3]).astype(jnp.bfloat16)
                    tall[j, 0, rows, :] = d[:, :pixels]
                    tall[j, 0, low(rows), :] = d[:, pixels:]
            for j in lanes_of:
                for rows in steps:
                    dr = dot(matrices[2, rows, :], tall[j, 0])
                    di = dot(matrices[2, low(rows), :], tall[j, 0])
                    wr, wi = wave1[first + j, rows, :pixels], wave1[first + j, rows, pixels:]
                    patch_grad[1, 0, rows, :] += dr * wr + di * wi
                    patch_grad[1, 1, rows, :] += di * wr - dr * wi
                    qr, qi = patch[1, 0, rows, :], patch[1, 1, rows, :]
                    wide[j, 0, rows, :pixels] = (dr * qr + di * qi).astype(jnp.bfloat16)
                    wide[j, 0, rows, pixels:] = (di * qr - dr * qi).astype(jnp.bfloat16)
            for j in lanes_of:
                for rows in steps:
                    d = dot(wide[j, 0, rows, :], matrices[1]).astype(jnp.bfloat16)
                    tall[j, 1, rows, :] = d[:, :pixels]
                    tall[j, 1, low(rows), :] = d[:, pixels:]
            for j in lanes_of:
                for rows in steps:
                    dr = dot(matrices[0, rows, :], tall[j, 1])
                    di = dot(matrices[0, low(rows), :], tall[j, 1])
                    pr, pi = load_probe(first + j, 0, rows), load_probe(first + j, 1, rows)
                    patch_grad[0, 0, rows, :] += dr * pr + di * pi
                    patch_grad[0, 1, rows, :] += di * pr - dr * pi
                    qr, qi = patch[0, 0, rows, :], patch[0, 1, rows, :]
                    for part, value in enumerate((dr * qr + di * qi, di * qr - dr * qi)):
                        window = window_of(first + j, part, rows)
                        probe_grad[0, window, :] += value[:, :half]
                        probe_grad[1, window, :] += value[:, half:]
            return 0

        lax.fori_loop(0, modes // GROUP, backward, 0)

        @pl.when(n == positions - 1)
        def _():
            lax.fori_loop(0, packed.shape[1], pack, 0, unroll=8)
            for copy in probe_out:
                copy.start()

        for k in range(2):
            for part in range(2):
                lane = (k * 2 + part) * 320 - part * 64
                for i in range(0, pixels, CUT):
                    piece = shift_right(patch_grad[k, part, i : i + CUT, :], column + part * 64, down)
                    window = pl.ds(pl.multiple_of(base + i, 8), CUT + 8)
                    canvas[place, window, lane : lane + 384] += piece
        return 0

    lax.fori_loop(0, positions, position, 0)
    for copy in canvas_out:
        copy.start()
    for copy in probe_out + canvas_out:
        copy.wait()


def device_gradients(offsets, chosen, mine, other, tile_parts, amplitudes):
    half = mine.shape[2]
    rows, pixels = mine.shape[0] * mine.shape[1], 2 * half
    modes = rows // (2 * pixels)
    positions = amplitudes.shape[0]
    scalar = pl.BlockSpec(memory_space=pltpu.SMEM)
    whole = pl.BlockSpec(memory_space=pltpu.VMEM)
    there = pl.BlockSpec(memory_space=pl.ANY)
    scratch = [
        pltpu.VMEM((2, rows, half), jnp.float32),
        pltpu.VMEM((4, 320, 1280), jnp.float32),
        pltpu.VMEM((2, rows, half), jnp.float32),
        pltpu.VMEM((positions, 2, 2, 320, 384), jnp.float32),
        pltpu.VMEM((2,) + mine.shape, jnp.float32),
        pltpu.VMEM((2, 2, pixels, pixels), jnp.float32),
        pltpu.VMEM((2, 2, pixels, pixels), jnp.float32),
        pltpu.VMEM((modes, pixels, 2 * pixels), jnp.float32),
        pltpu.VMEM((modes, pixels, 2 * pixels), jnp.float32),
        pltpu.VMEM((GROUP, 2, 2 * pixels, pixels), jnp.bfloat16),
        pltpu.VMEM((GROUP, 2, pixels, 2 * pixels), jnp.bfloat16),
        pltpu.VMEM((pixels, pixels), jnp.float32),
        pltpu.SemaphoreType.DMA((2,)),
        pltpu.SemaphoreType.DMA((positions, 2)),
        pltpu.SemaphoreType.DMA((2, 2, 18)),
    ]
    flops = positions * modes * 8 * 4 * 2 * pixels**3
    return pl.pallas_call(
        kernel,
        out_shape=(jax.ShapeDtypeStruct((16, 592, 128), jnp.float32),) * 2,
        in_specs=[scalar] * 2 + [there] * 8 + [whole] * 2,
        out_specs=(there, there),
        scratch_shapes=scratch,
        cost_estimate=pl.CostEstimate(flops=flops, bytes_accessed=20_000_000, transcendentals=0),
        compiler_params=pltpu.CompilerParams(vmem_limit_bytes=56 * 1024 * 1024),
        name="gradients",
    )(offsets, chosen, mine, other, *tile_parts, amplitudes, jnp.asarray(block_matrices(pixels)))


def exchange(value, axes):
    return lax.all_to_all(value, axes, split_axis=0, concat_axis=0, tiled=True)


def spread(value, axes, count):
    return exchange(jnp.broadcast_to(value[None], (count,) + value.shape), axes)


def reduce_over(value, axes):
    return jnp.sum(exchange(value, axes), axis=0)


def shift(value, axes, count, by):
    return lax.ppermute(value, axes, [(i, (i + by) % count) for i in range(count)])


def device_body(probe_modes, object_tiles, scan_offsets, patch_tiles, amplitudes):
    own_rows, pixels = probe_modes.shape
    half = pixels // 2

    padded = jnp.pad(object_tiles[0], ((0, 0), (0, 0), (0, 0), (0, 64)))
    far0 = shift(padded[0], ("yh", "yl"), 4, 1)
    far1 = shift(padded[1], ("yh", "yl"), 4, 3)
    partner = shift(padded, "c", 2, 1)
    cross0 = shift(far0, "c", 2, 1)
    cross1 = shift(far1, "c", 2, 1)

    first = lax.axis_index("c") == 0
    eight = jnp.where(first, probe_modes[:8], probe_modes[4:])
    four = jnp.where(first, probe_modes[8:], probe_modes[:4])
    mixed = (four[:, :half], four[:, half:])
    mixed = jnp.where(first, jnp.concatenate(mixed), jnp.concatenate(mixed[::-1]))
    piece = jnp.concatenate([eight[:, :half], eight[:, half:], mixed])
    block = spread(piece, ("yh", "z", "yl"), 32)
    mine = spread(block, "x", 4).reshape(128, 2 * own_rows, half)
    other = shift(mine, "c", 2, 1)

    keep, send = device_gradients(
        scan_offsets,
        patch_tiles,
        mine,
        other,
        (padded, partner, far0, far1, cross0, cross1),
        amplitudes,
    )

    total = keep + shift(send, "c", 2, 1)
    total = reduce_over(total, ("yl", "x", "yh"))
    objects = total[:400].reshape(10, 8, 5, 128).transpose(1, 0, 2, 3).reshape(8, 50, 128)
    total = reduce_over(jnp.concatenate([objects, total[400:].reshape(8, 24, 128)], axis=1), "z")
    object_gradient = total[:50].reshape(10, 5, 128).transpose(1, 0, 2).reshape(5, 2, 2, 320)
    object_gradient = object_gradient.transpose(1, 2, 0, 3)[None]
    piece = total[50:]
    eight = jnp.concatenate([piece[:8], piece[8:16]], axis=1)
    four = jnp.where(
        first,
        jnp.concatenate([piece[16:20], piece[20:]], axis=1),
        jnp.concatenate([piece[20:], piece[16:20]], axis=1),
    )
    probe_gradient = jnp.where(first, jnp.concatenate([eight, four]), jnp.concatenate([four, eight]))
    return (probe_gradient, object_gradient)


def solution(mesh):
    fine = Mesh(mesh.devices.reshape(4, 2, 8, 2, 2), AXES)
    scan, tile = AXES[:3], AXES[3:]
    placed = (
        P(AXES, None),
        P(tile, None, None, None, None),
        P(AXES, None),
        P(AXES),
        P(AXES, None, None),
    )
    return jax.shard_map(
        device_body,
        mesh=fine,
        in_specs=placed,
        out_specs=(P(AXES, None), P(tile, None, None, scan, None)),
        check_vma=False,
    )
```

```python
import math

import jax
import jax.numpy as jnp
import numpy as np
from jax import lax
from jax.experimental import pallas as pl
from jax.experimental.pallas import tpu as pltpu
from jax.sharding import Mesh
from jax.sharding import PartitionSpec as P

AXES = ("x", "yh", "z", "yl", "c")
ROWS = 256
CUT = 64
GROUP = 2


def block_matrices(pixels):
    index = np.arange(pixels, dtype=np.int64)
    chirp = ((index[:, None] - index[None, :]) ** 2 % (2 * pixels)) * (math.pi / pixels)
    turn = (index[:, None] * index[None, :] % pixels) * (2.0 * math.pi / pixels)
    scale = 1.0 / math.sqrt(pixels)
    result = []
    for re, im in ((np.cos(chirp), np.sin(chirp)), (np.cos(turn), -np.sin(turn))):
        re, im = (re * scale).astype(jnp.bfloat16), (im * scale).astype(jnp.bfloat16)
        result.append(np.block([[re, im], [-im, re]]))
        result.append(np.block([[re, -im], [im, re]]))
    return np.stack(result)


def dot(a, b):
    return jnp.dot(a, b, preferred_element_type=jnp.float32)


def shift_left(value, lanes, sublanes):
    groups = value.shape[0] // 8
    value = pltpu.roll(value.reshape(groups, 8, 384), lax.rem(8 - sublanes, 8), 1)
    index = lax.broadcasted_iota(jnp.int32, (groups - 1, 8, 384), 1)
    value = jnp.where(index < 8 - sublanes, value[:-1], value[1:]).reshape(8 * groups - 8, 384)
    turn = lax.rem(128 - lanes, 128)
    parts = [pltpu.roll(value[:, a : a + 128], turn, 1) for a in (0, 128, 256)]
    index = lax.broadcasted_iota(jnp.int32, parts[0].shape, 1)
    keep = index < 128 - lanes
    return jnp.concatenate([jnp.where(keep, a, b) for a, b in zip(parts, parts[1:])], axis=1)


def shift_right(value, lanes, sublanes):
    groups = value.shape[0] // 8
    turn = lax.rem(lanes, 128)
    zero = jnp.zeros((value.shape[0], 128), jnp.float32)
    parts = [zero] + [pltpu.roll(value[:, a : a + 128], turn, 1) for a in (0, 128)] + [zero]
    index = lax.broadcasted_iota(jnp.int32, zero.shape, 1)
    moved = index < lanes
    value = jnp.concatenate([jnp.where(moved, a, b) for a, b in zip(parts, parts[1:])], axis=1)
    value = pltpu.roll(value.reshape(groups, 8, 384), lax.rem(sublanes, 8), 1)
    zero = jnp.zeros((1, 8, 384), jnp.float32)
    above, below = jnp.concatenate([zero, value]), jnp.concatenate([value, zero])
    index = lax.broadcasted_iota(jnp.int32, above.shape, 1)
    return jnp.where(index < sublanes, above, below).reshape(8 * groups + 8, 384)


def kernel(
    offsets,
    chosen,
    mine,
    other,
    own,
    partner,
    far0,
    far1,
    cross0,
    cross1,
    amplitudes,
    matrices,
    keep,
    send,
    probe_grad,
    canvas,
    probe,
    tiles,
    packed,
    patch,
    patch_grad,
    wave1,
    wave2,
    tall,
    wide,
    intensity,
    probe_sem,
    tile_sem,
    out_sem,
):
    half = probe_grad.shape[2]
    pixels = 2 * half
    modes = wave1.shape[0]
    positions = tiles.shape[0]
    core, low_y = lax.axis_index("c"), lax.axis_index("yl")
    steps = [slice(i, i + ROWS) for i in range(0, pixels, ROWS)]
    lanes_of = range(GROUP)

    def low(rows):
        return slice(rows.start + pixels, rows.stop + pixels)

    blocks = packed.reshape(2, 8, 8, 2, 24, half)
    copies = [
        pltpu.make_async_copy(source.at[:, y], blocks.at[side, :, :, y], probe_sem.at[i, y])
        for i, (source, side) in enumerate(((mine, core), (other, 1 - core)))
        for y in range(2)
    ]
    for copy in copies:
        copy.start()
    grad_blocks = packed.reshape(2, 8, 8, 2, 24, half)
    probe_out = [
        pltpu.make_async_copy(
            grad_blocks.at[side, :, z, y],
            target.at[8 * y : 8 * y + 8, 400 + 24 * z : 424 + 24 * z, :],
            out_sem.at[i, y, z],
        )
        for i, (target, side) in enumerate(((keep, core), (send, 1 - core)))
        for y in range(2)
        for z in range(8)
    ]
    canvas_blocks = canvas.reshape(4, 8, 40, 1280)
    canvas_out = [
        pltpu.make_async_copy(
            canvas_blocks.at[2 * i + y, :, :, 128 * j : 128 * j + 128],
            target.at[8 * y : 8 * y + 8, 40 * j : 40 * j + 40, :],
            out_sem.at[i, y, 8 + j],
        )
        for i, target in enumerate((keep, send))
        for y in range(2)
        for j in range(10)
    ]
    for n in range(positions):
        tile = chosen[n]
        kind = 2 * (lax.div(tile, 2) ^ low_y) + (lax.rem(tile, 2) ^ core)
        for source, (first, second) in enumerate(
            ((own.at[0], own.at[1]), (partner.at[0], partner.at[1]), (far0, far1), (cross0, cross1))
        ):

            @pl.when(kind == source)
            def _():
                pltpu.make_async_copy(first, tiles.at[n, 0], tile_sem.at[n, 0]).start()
                pltpu.make_async_copy(second, tiles.at[n, 1], tile_sem.at[n, 1]).start()

    canvas[...] = jnp.zeros_like(canvas)
    probe_grad[...] = jnp.zeros_like(probe_grad)
    for n in range(positions):
        for k in range(2):
            pltpu.make_async_copy(far0, tiles.at[n, k], tile_sem.at[n, k]).wait()
    for copy in copies:
        copy.wait()
    upper = lax.broadcasted_iota(jnp.int32, (8, half), 0) < 4

    def unpack(block, _):
        start = pl.multiple_of(24 * block, 8)
        for side in range(2):
            probe[side, pl.ds(start, 8), :] = packed[0, block, 8 * side : 8 * side + 8, :]
            probe[side, pl.ds(start + 16, 8), :] = packed[1, block, 8 * side : 8 * side + 8, :]
        a, b = packed[0, block, 16:24, :], packed[1, block, 16:24, :]
        probe[0, pl.ds(start + 8, 8), :] = jnp.where(upper, a, b)
        probe[1, pl.ds(start + 8, 8), :] = pltpu.roll(jnp.where(upper, b, a), 4, 0)
        return 0

    def pack(block, _):
        start = pl.multiple_of(24 * block, 8)
        for side in range(2):
            packed[0, block, 8 * side : 8 * side + 8, :] = probe_grad[side, pl.ds(start, 8), :]
            packed[1, block, 8 * side : 8 * side + 8, :] = probe_grad[side, pl.ds(start + 16, 8), :]
        a = probe_grad[0, pl.ds(start + 8, 8), :]
        b = pltpu.roll(probe_grad[1, pl.ds(start + 8, 8), :], 4, 0)
        packed[0, block, 16:24, :] = jnp.where(upper, a, b)
        packed[1, block, 16:24, :] = jnp.where(upper, b, a)
        return 0

    lax.fori_loop(0, packed.shape[1], unpack, 0, unroll=8)

    def window_of(m, part, rows):
        start = pl.multiple_of((part * modes + m) * pixels, pixels) + rows.start
        return pl.ds(pl.multiple_of(start, ROWS), ROWS)

    def load_probe(m, part, rows):
        window = window_of(m, part, rows)
        return jnp.concatenate([probe[0, window, :], probe[1, window, :]], axis=1)

    def position(n, _):
        row, column, tile = offsets[n, 0], offsets[n, 1], chosen[n]
        base = jnp.minimum(lax.div(row, 8) * 8, 56)
        down = row - base
        place = 2 * (lax.rem(tile, 2) ^ core) + lax.div(tile, 2)
        for k in range(2):
            for part in range(2):
                for i in range(0, pixels, CUT):
                    window = pl.ds(pl.multiple_of(base + i, 8), CUT + 8)
                    piece = tiles[n, k, window, 256 * part : 256 * part + 384]
                    patch[k, part, i : i + CUT, :] = shift_left(piece, column + 64 * part, down)
        patch_grad[...] = jnp.zeros_like(patch_grad)
        intensity[...] = jnp.zeros_like(intensity)

        def forward(group, _):
            first = group * GROUP
            for j in lanes_of:
                for rows in steps:
                    pr, pi = load_probe(first + j, 0, rows), load_probe(first + j, 1, rows)
                    qr, qi = patch[0, 0, rows, :], patch[0, 1, rows, :]
                    tall[j, 0, rows, :] = (pr * qr - pi * qi).astype(jnp.bfloat16)
                    tall[j, 0, low(rows), :] = (pr * qi + pi * qr).astype(jnp.bfloat16)
            for j in lanes_of:
                for rows in steps:
                    a = dot(matrices[1, rows, :], tall[j, 0])
                    wide[j, 0, rows, :pixels] = a.astype(jnp.bfloat16)
                    a = dot(matrices[1, low(rows), :], tall[j, 0])
                    wide[j, 0, rows, pixels:] = a.astype(jnp.bfloat16)
            for j in lanes_of:
                for rows in steps:
                    w = dot(wide[j, 0, rows, :], matrices[0])
                    wave1[first + j, rows, :] = w
                    wr, wi = w[:, :pixels], w[:, pixels:]
                    qr, qi = patch[1, 0, rows, :], patch[1, 1, rows, :]
                    tall[j, 1, rows, :] = (wr * qr - wi * qi).astype(jnp.bfloat16)
                    tall[j, 1, low(rows), :] = (wr * qi + wi * qr).astype(jnp.bfloat16)
            for j in lanes_of:
                for rows in steps:
                    a = dot(matrices[3, rows, :], tall[j, 1])
                    wide[j, 1, rows, :pixels] = a.astype(jnp.bfloat16)
                    a = dot(matrices[3, low(rows), :], tall[j, 1])
                    wide[j, 1, rows, pixels:] = a.astype(jnp.bfloat16)
            for j in lanes_of:
                for rows in steps:
                    w = dot(wide[j, 1, rows, :], matrices[2])
                    wave2[first + j, rows, :] = w
                    wr, wi = w[:, :pixels], w[:, pixels:]
                    intensity[rows, :] += wr * wr + wi * wi
            return 0

        lax.fori_loop(0, modes // GROUP, forward, 0)
        for rows in steps:
            measured = amplitudes[n, rows, :].astype(jnp.float32)
            intensity[rows, :] = 2.0 - 2.0 * measured * lax.rsqrt(intensity[rows, :] + 1.0)

        def backward(group, _):
            first = group * GROUP
            for j in lanes_of:
                for rows in steps:
                    g = intensity[rows, :]
                    w = wave2[first + j, rows, :]
                    d = (w * jnp.concatenate([g, g], axis=1)).astype(jnp.bfloat16)
                    d = dot(d, matrices[3]).astype(jnp.bfloat16)
                    tall[j, 0, rows, :] = d[:, :pixels]
                    tall[j, 0, low(rows), :] = d[:, pixels:]
            for j in lanes_of:
                for rows in steps:
                    dr = dot(matrices[2, rows, :], tall[j, 0])
                    di = dot(matrices[2, low(rows), :], tall[j, 0])
                    wr, wi = wave1[first + j, rows, :pixels], wave1[first + j, rows, pixels:]
                    patch_grad[1, 0, rows, :] += dr * wr + di * wi
                    patch_grad[1, 1, rows, :] += di * wr - dr * wi
                    qr, qi = patch[1, 0, rows, :], patch[1, 1, rows, :]
                    wide[j, 0, rows, :pixels] = (dr * qr + di * qi).astype(jnp.bfloat16)
                    wide[j, 0, rows, pixels:] = (di * qr - dr * qi).astype(jnp.bfloat16)
            for j in lanes_of:
                for rows in steps:
                    d = dot(wide[j, 0, rows, :], matrices[1]).astype(jnp.bfloat16)
                    tall[j, 1, rows, :] = d[:, :pixels]
                    tall[j, 1, low(rows), :] = d[:, pixels:]
            for j in lanes_of:
                for rows in steps:
                    dr = dot(matrices[0, rows, :], tall[j, 1])
                    di = dot(matrices[0, low(rows), :], tall[j, 1])
                    pr, pi = load_probe(first + j, 0, rows), load_probe(first + j, 1, rows)
                    patch_grad[0, 0, rows, :] += dr * pr + di * pi
                    patch_grad[0, 1, rows, :] += di * pr - dr * pi
                    qr, qi = patch[0, 0, rows, :], patch[0, 1, rows, :]
                    for part, value in enumerate((dr * qr + di * qi, di * qr - dr * qi)):
                        window = window_of(first + j, part, rows)
                        probe_grad[0, window, :] += value[:, :half]
                        probe_grad[1, window, :] += value[:, half:]
            return 0

        lax.fori_loop(0, modes // GROUP, backward, 0)

        @pl.when(n == positions - 1)
        def _():
            lax.fori_loop(0, packed.shape[1], pack, 0, unroll=8)
            for copy in probe_out:
                copy.start()

        for k in range(2):
            for part in range(2):
                lane = (k * 2 + part) * 320 - part * 64
                for i in range(0, pixels, CUT):
                    piece = shift_right(patch_grad[k, part, i : i + CUT, :], column + part * 64, down)
                    window = pl.ds(pl.multiple_of(base + i, 8), CUT + 8)
                    canvas[place, window, lane : lane + 384] += piece
        return 0

    lax.fori_loop(0, positions, position, 0)
    for copy in canvas_out:
        copy.start()
    for copy in probe_out + canvas_out:
        copy.wait()


def device_gradients(offsets, chosen, mine, other, tile_parts, amplitudes):
    half = mine.shape[-1]
    rows, pixels = math.prod(mine.shape[:-1]), 2 * half
    modes = rows // (2 * pixels)
    positions = amplitudes.shape[0]
    scalar = pl.BlockSpec(memory_space=pltpu.SMEM)
    whole = pl.BlockSpec(memory_space=pltpu.VMEM)
    there = pl.BlockSpec(memory_space=pl.ANY)
    scratch = [
        pltpu.VMEM((2, rows, half), jnp.float32),
        pltpu.VMEM((4, 320, 1280), jnp.float32),
        pltpu.VMEM((2, rows, half), jnp.float32),
        pltpu.VMEM((positions, 2, 320, 640), jnp.float32),
        pltpu.VMEM((2, rows // 24, 24, half), jnp.float32),
        pltpu.VMEM((2, 2, pixels, pixels), jnp.float32),
        pltpu.VMEM((2, 2, pixels, pixels), jnp.float32),
        pltpu.VMEM((modes, pixels, 2 * pixels), jnp.float32),
        pltpu.VMEM((modes, pixels, 2 * pixels), jnp.float32),
        pltpu.VMEM((GROUP, 2, 2 * pixels, pixels), jnp.bfloat16),
        pltpu.VMEM((GROUP, 2, pixels, 2 * pixels), jnp.bfloat16),
        pltpu.VMEM((pixels, pixels), jnp.float32),
        pltpu.SemaphoreType.DMA((2, 2)),
        pltpu.SemaphoreType.DMA((positions, 2)),
        pltpu.SemaphoreType.DMA((2, 2, 18)),
    ]
    flops = positions * modes * 8 * 4 * 2 * pixels**3
    return pl.pallas_call(
        kernel,
        out_shape=(jax.ShapeDtypeStruct((16, 592, 128), jnp.float32),) * 2,
        in_specs=[scalar] * 2 + [there] * 8 + [whole] * 2,
        out_specs=(there, there),
        scratch_shapes=scratch,
        cost_estimate=pl.CostEstimate(flops=flops, bytes_accessed=20_000_000, transcendentals=0),
        compiler_params=pltpu.CompilerParams(vmem_limit_bytes=40 * 1024 * 1024),
        name="gradients",
    )(offsets, chosen, mine, other, *tile_parts, amplitudes, jnp.asarray(block_matrices(pixels)))


def exchange(value, axes):
    return lax.all_to_all(value, axes, split_axis=0, concat_axis=0, tiled=True)


def spread(value, axes, count):
    return exchange(jnp.broadcast_to(value[None], (count,) + value.shape), axes)


def reduce_over(value, axes):
    return jnp.sum(exchange(value, axes), axis=0)


def shift(value, axes, count, by):
    return lax.ppermute(value, axes, [(i, (i + by) % count) for i in range(count)])


def device_body(probe_modes, object_tiles, scan_offsets, patch_tiles, amplitudes):
    own_rows, pixels = probe_modes.shape
    half = pixels // 2

    joined = jnp.concatenate([object_tiles[0, :, 0], object_tiles[0, :, 1]], axis=2)
    far0 = shift(joined[0], ("yh", "yl"), 4, 1)
    far1 = shift(joined[1], ("yh", "yl"), 4, 3)
    partner = shift(joined, "c", 2, 1)
    zero = probe_modes[0, 0] * 0.0
    relay0 = far0 + zero
    relay1 = far1 + zero
    cross0 = shift(relay0, "c", 2, 1)
    cross1 = shift(relay1, "c", 2, 1)

    first = lax.axis_index("c") == 0
    eight = jnp.where(first, probe_modes[:8], probe_modes[4:])
    four = jnp.where(first, probe_modes[8:], probe_modes[:4])
    mixed = (four[:, :half], four[:, half:])
    mixed = jnp.where(first, jnp.concatenate(mixed), jnp.concatenate(mixed[::-1]))
    piece = jnp.concatenate([eight[:, :half], eight[:, half:], mixed])
    block = spread(piece, "z", 8)
    mine = spread(block, ("x", "yh", "yl"), 16).reshape(8, 2, 8, 2 * own_rows, half)
    other = shift(mine, "c", 2, 1)

    keep, send = device_gradients(
        scan_offsets,
        patch_tiles,
        mine,
        other,
        (joined, partner, far0, far1, cross0, cross1),
        amplitudes,
    )

    total = keep + shift(send, "c", 2, 1)
    total = reduce_over(total, ("yl", "x", "yh"))
    objects = total[:400].reshape(10, 8, 5, 128).transpose(1, 0, 2, 3).reshape(8, 50, 128)
    total = reduce_over(jnp.concatenate([objects, total[400:].reshape(8, 24, 128)], axis=1), "z")
    object_gradient = total[:50].reshape(10, 5, 128).transpose(1, 0, 2).reshape(5, 2, 2, 320)
    object_gradient = object_gradient.transpose(1, 2, 0, 3)[None]
    piece = total[50:]
    eight = jnp.concatenate([piece[:8], piece[8:16]], axis=1)
    four = jnp.where(
        first,
        jnp.concatenate([piece[16:20], piece[20:]], axis=1),
        jnp.concatenate([piece[20:], piece[16:20]], axis=1),
    )
    probe_gradient = jnp.where(first, jnp.concatenate([eight, four]), jnp.concatenate([four, eight]))
    return (probe_gradient, object_gradient)


def solution(mesh):
    fine = Mesh(mesh.devices.reshape(4, 2, 8, 2, 2), AXES)
    scan, tile = AXES[:3], AXES[3:]
    placed = (
        P(AXES, None),
        P(tile, None, None, None, None),
        P(AXES, None),
        P(AXES),
        P(AXES, None, None),
    )
    return jax.shard_map(
        device_body,
        mesh=fine,
        in_specs=placed,
        out_specs=(P(AXES, None), P(tile, None, None, scan, None)),
        check_vma=False,
    )
```
